32 devices in a mesh: groups: 2 (over x), blk: 16 (over z, y, core).
Axes of the slice: x: 2, y: 2, z: 4, core: 2. Of those that a mesh axis runs over, the one named last changes fastest.
Arguments:
- queries: bfloat16 [24576, 1536], P(('groups', 'blk')), parts along dimension 0, may hold values from -20 to 20
- keys: bfloat16 [24576, 1536], P(('groups', 'blk')), parts along dimension 0, may hold values from -6 to 6
- values: bfloat16 [24576, 1536], P(('groups', 'blk')), parts along dimension 0, may hold values from -6 to 6
- neighbours: int32 [64, 7], P(('groups', 'blk')), parts along dimension 0, may hold values from -1 to 31, as said below
Outputs:
- attended: bfloat16 [24576, 1536], P(('groups', 'blk')), parts along dimension 0
The draws below stay inside these ranges and needn't reach their ends.
There are 2 independent parts, one for each index of `groups`. The reference program is written for one: setup_inputs(seed, part) draws one part's arguments, and reference() takes and returns one part's arrays. A program takes and returns all parts, laid end to end along the dimension named above; each array names one. Nothing has to cross between parts.
Inputs may be any that keep to these rules, and one draw needn't show every extreme that they name: `neighbours`: entry 0 of row t is t itself. Every other non-negative entry names a distinct tile of a frame block at most two blocks away from tile t's block; a slot is -1 only where its drawn tile falls outside the clip.
All inputs are finite; a program needn't handle non-finite values.
Results may differ from the reference program's by a relative error of at most 0.0048.
Values may be sent and summed in bfloat16 or wider, within the bound.
A program may use at most 128 MiB of HBM per device.

```python
import jax
import jax.numpy as jnp
from jax import lax

HEADS = 12
HD = 128
TILE = 384
NBR = 7
TILES_DEV = 2
TILES = 32
TOKENS = 12288


def query_key_pair(key):
    query_key = jax.random.fold_in(key, 11)
    key_key = jax.random.fold_in(key, 12)
    shape = (TOKENS, HEADS * HD)
    keys_drawn = jnp.clip(jax.random.normal(key_key, shape, jnp.float32), -6.0, 6.0)
    queries_drawn = jnp.clip(jax.random.normal(query_key, shape, jnp.float32), -6.0, 6.0)
    return (queries_drawn, keys_drawn)


def draw_queries(key, part):
    return query_key_pair(key)[0].astype(jnp.bfloat16)


def draw_keys(key, part):
    return query_key_pair(key)[1].astype(jnp.bfloat16)


def draw_neighbours(key, part):
    candidates = 5 * TILES_DEV
    rows = jnp.arange(TILES, dtype=jnp.int32)
    block = rows // TILES_DEV
    base = (block - 2) * TILES_DEV
    own_offset = rows - base
    row_keys = jax.random.split(jax.random.fold_in(key, 21), TILES)
    picks = jax.vmap(lambda row_key: jax.random.permutation(row_key, candidates - 1))(row_keys)[:, :NBR - 1]
    offsets = picks + (picks >= own_offset[:, None]).astype(jnp.int32)
    others = base[:, None] + offsets
    others = jnp.where((others >= 0) & (others < TILES), others, -1)
    return jnp.concatenate([rows[:, None], others], axis=1).astype(jnp.int32)


def level_of(own_key, extent, cuts, low, largest):
    def one(dim, parts):
        steps = jax.random.uniform(jax.random.fold_in(jax.random.fold_in(own_key, 6), dim), (parts,), jnp.float32, low / len(cuts), largest / len(cuts))
        return jnp.repeat(jnp.exp(steps), extent[dim] // parts).reshape((-1,) + (1,) * (len(extent) - dim - 1))

    loudness = one(*cuts[0])
    for cut in cuts[1:]:
        loudness = loudness * one(*cut)
    return loudness


def scatter_about(stream_key, extent, deviation, most, cuts=(), kind=jnp.bfloat16):
    loudness = level_of(stream_key, extent, cuts, -0.22, 0.18) if cuts else 1.0
    array = jax.random.normal(stream_key, extent, jnp.float32) * deviation * loudness
    return jnp.minimum(jnp.maximum(array, -most), most).astype(kind)


def setup_inputs(seed: int = 0, part: int = 0) -> dict:
    arg_keys = jax.random.split(jax.random.key(seed), 5)
    part_splits = jax.random.split(jax.random.fold_in(arg_keys[4], part), 5)
    return {
        "queries": draw_queries(jax.random.fold_in(jax.random.fold_in(arg_keys[4], part), 71), part),
        "keys": draw_keys(jax.random.fold_in(jax.random.fold_in(arg_keys[4], part), 71), part),
        "values": scatter_about(part_splits[2], (TOKENS, HEADS * HD), 1.0, 6.0, ((0, 16),)),
        "neighbours": draw_neighbours(jax.random.fold_in(jax.random.fold_in(arg_keys[4], part), 71), part),
    }


def reference(queries, keys, values, neighbours):
    scale = HD ** -0.5
    q_tiles = queries.reshape(TILES, TILE, HEADS, HD)
    k_tiles = keys.reshape(TILES, TILE, HEADS, HD)
    v_tiles = values.reshape(TILES, TILE, HEADS, HD)

    def one_tile(tile_id):
        named = neighbours[tile_id]
        valid = named >= 0
        safe = jnp.where(valid, named, 0).astype(jnp.int32)
        key_rows = k_tiles[safe].reshape(NBR * TILE, HEADS, HD).astype(jnp.float32)
        value_rows = v_tiles[safe].reshape(NBR * TILE, HEADS, HD).astype(jnp.float32)
        query_rows = q_tiles[tile_id].astype(jnp.float32)
        scores = jnp.einsum("qhd,khd->hqk", query_rows, key_rows) * scale
        key_mask = jnp.repeat(valid, TILE)
        scores = jnp.where(key_mask[None, None, :], scores, -jnp.inf)
        peak = jnp.max(scores, axis=2, keepdims=True)
        weights = jnp.exp(scores - peak)
        total = jnp.sum(weights, axis=2)
        rounded = lax.optimization_barrier(weights.astype(jnp.bfloat16)).astype(jnp.float32)
        summed = jnp.einsum("hqk,khd->qhd", rounded, value_rows)
        result = summed / jnp.transpose(total)[:, :, None]
        return result.astype(jnp.bfloat16).reshape(TILE, HEADS * HD)

    output = lax.map(one_tile, jnp.arange(TILES, dtype=jnp.int32))
    return output.reshape(TILES * TILE, HEADS * HD)
```

```python
import functools
import math

import jax
import jax.numpy as jnp
from jax import lax
from jax.experimental import pallas as pl
from jax.experimental.pallas import tpu as pltpu
from jax.sharding import PartitionSpec as P

HD = 128
WINDOW = 5
ROWS = 384


def kernel(count, heads, named, queries, keys, values, out, *scratch):
    windows = (scratch[:heads], scratch[heads : 2 * heads])
    (held_q, held_o, local_sem, q_sem, o_sem, y_send, y_recv, sib_send, sib_recv,
     z_send, z_recv, share_send, share_recv) = scratch[2 * heads :]
    sources = (keys, values)
    tiles, tile_len, _ = queries.shape
    slots = named.shape[1]
    rows = min(ROWS, tile_len)
    factor = math.log2(math.e) * HD ** -0.5

    me = lax.axis_index("blk")
    core = lax.rem(me, 2)
    side = lax.rem(me // 2, 2)
    quad = me // 4
    last = count // 4 - 1
    sibling = me + 1 - 2 * core
    partner = me + 2 - 4 * side
    ahead = me + 4 - 8 * side
    can_relay = jnp.where(side == 0, quad < last, quad > 0)
    gets_relay = jnp.where(side == 0, quad > 0, quad < last)
    shares_partner = core == side
    partner_at = 4 - 4 * side
    relay_at = 4 * side

    def part(ref, block):
        return ref.at[pl.ds(block * tiles, tiles)]

    def columns(ref, head):
        return ref.at[:, :, pl.ds(head * HD, HD)]

    def local_copy(head, which):
        return pltpu.make_async_copy(
            columns(sources[which], head), part(windows[which][head], 2), local_sem.at[head, which]
        )

    def remote(src, dst, send, recv, head, which, target):
        return pltpu.make_async_remote_copy(
            src_ref=src, dst_ref=dst, send_sem=send.at[head, which], recv_sem=recv.at[head, which],
            device_id={"blk": target}, device_id_type=pl.DeviceIdType.MESH,
        )

    def partner_copy(head, which):
        return remote(columns(sources[which], head), part(windows[which][head], relay_at),
                      y_send, y_recv, head, which, partner)

    def sibling_copy(head, which):
        return remote(columns(sources[which], head), part(windows[which][head], 1 + 2 * core),
                      sib_send, sib_recv, head, which, sibling)

    def relay_copy(head, which):
        window = windows[which][head]
        return remote(part(window, partner_at), part(window, relay_at),
                      z_send, z_recv, head, which, ahead)

    def share_copy(head, which):
        window = windows[which][head]
        return remote(part(window, 4 - 4 * core), part(window, 3 - 2 * core),
                      share_send, share_recv, head, which, sibling)

    def query_copy(head):
        return pltpu.make_async_copy(columns(queries, head), columns(held_q, head), q_sem.at[head])

    def out_copy(head):
        return pltpu.make_async_copy(columns(held_o, head), columns(out, head), o_sem.at[head])

    barrier = pltpu.get_barrier_semaphore()

    def greet(target):
        pl.semaphore_signal(barrier, inc=1, device_id={"blk": target}, device_id_type=pl.DeviceIdType.MESH)

    greet(sibling)
    greet(partner)

    @pl.when(quad > 0)
    def _():
        greet(me - 4)

    @pl.when(quad < last)
    def _():
        greet(me + 4)

    pl.semaphore_wait(barrier, 2 + (quad > 0).astype(jnp.int32) + (quad < last).astype(jnp.int32))

    for head in range(heads):
        for which in range(2):
            partner_copy(head, which).start()
        for which in range(2):
            sibling_copy(head, which).start()
            local_copy(head, which).start()
        query_copy(head).start()

    def attend(head):
        key_window, value_window = windows[0][head], windows[1][head]
        start = head * HD
        per_tile = tile_len // rows

        def block(index, carry):
            tile = index // per_tile
            row = pl.multiple_of(lax.rem(index, per_tile) * rows, rows)
            query = held_q[tile, pl.ds(row, rows), start : start + HD]
            own = 2 * tiles + tile
            base = (me - 2) * tiles
            scores, peaks, valid, places = [], [], [], []
            for slot in range(slots):
                entry = named[tile, slot]
                ok = entry >= 0
                place = jnp.clip(jnp.where(ok, entry - base, own), 0, WINDOW * tiles - 1)
                score = lax.dot_general(
                    query, key_window[place], (((1,), (1,)), ((), ())),
                    preferred_element_type=jnp.float32,
                )
                peak = jnp.max(score, axis=1, keepdims=True)
                peaks.append(jnp.where(ok, peak, -jnp.inf))
                scores.append(score)
                valid.append(ok)
                places.append(place)
            top = functools.reduce(jnp.maximum, peaks) * factor
            total = jnp.zeros((rows, 1), jnp.float32)
            summed = jnp.zeros((rows, HD), jnp.float32)
            for slot in range(slots):
                offset = jnp.where(valid[slot], top, jnp.inf)
                weights = jnp.exp2(scores[slot] * factor - offset)
                total += jnp.sum(weights, axis=1, keepdims=True)
                summed += jnp.dot(
                    weights.astype(jnp.bfloat16), value_window[places[slot]],
                    preferred_element_type=jnp.float32,
                )
            held_o[tile, pl.ds(row, rows), start : start + HD] = (summed / total).astype(held_o.dtype)
            return carry

        lax.fori_loop(0, tiles * per_tile, block, 0)

    for step in range(heads + 1):
        if step < heads:
            for which in range(2):
                partner_copy(step, which).wait_recv()

                @pl.when(can_relay)
                def _():
                    relay_copy(step, which).start()

                @pl.when(shares_partner)
                def _():
                    share_copy(step, which).start()

        if step > 0:
            head = step - 1
            for which in range(2):

                @pl.when(gets_relay)
                def _():
                    relay_copy(head, which).wait_recv()

                    @pl.when(jnp.logical_not(shares_partner))
                    def _():
                        share_copy(head, which).start()

            query_copy(head).wait()
            for which in range(2):
                local_copy(head, which).wait()
                sibling_copy(head, which).wait_recv()

                @pl.when(jnp.logical_or(jnp.logical_not(shares_partner), gets_relay))
                def _():
                    share_copy(head, which).wait_recv()

            attend(head)
            out_copy(head).start()

    for head in range(heads):
        out_copy(head).wait()
        for which in range(2):
            partner_copy(head, which).wait_send()
            sibling_copy(head, which).wait_send()

            @pl.when(can_relay)
            def _():
                relay_copy(head, which).wait_send()

            @pl.when(jnp.logical_or(shares_partner, gets_relay))
            def _():
                share_copy(head, which).wait_send()


def on_device(count, queries, keys, values, neighbours):
    tokens, width = queries.shape
    tiles = neighbours.shape[0]
    tile_len = tokens // tiles
    heads = width // HD
    shape = (tiles, tile_len, width)
    window = pltpu.VMEM((WINDOW * tiles, tile_len, HD), queries.dtype)
    pair = pltpu.SemaphoreType.DMA((heads, 2))
    single = pltpu.SemaphoreType.DMA((heads,))
    hbm = pl.BlockSpec(memory_space=pl.ANY)
    out = pl.pallas_call(
        functools.partial(kernel, count, heads),
        out_shape=jax.ShapeDtypeStruct(shape, queries.dtype),
        in_specs=[pl.BlockSpec(memory_space=pltpu.SMEM), hbm, hbm, hbm],
        out_specs=hbm,
        scratch_shapes=[window] * (2 * heads)
        + [pltpu.VMEM(shape, queries.dtype)] * 2
        + [pair, single, single]
        + [pair] * 8,
        compiler_params=pltpu.CompilerParams(
            collective_id=0, has_side_effects=True, vmem_limit_bytes=60 * 1024 * 1024
        ),
    )(neighbours, queries.reshape(shape), keys.reshape(shape), values.reshape(shape))
    return out.reshape(tokens, width)


def solution(mesh):
    spec = P(("groups", "blk"), None)
    return jax.shard_map(
        functools.partial(on_device, mesh.shape["blk"]),
        mesh=mesh, in_specs=(spec,) * 4, out_specs=spec, check_vma=False,
    )
```

```python
import functools
import math

import jax
import jax.numpy as jnp
from jax import lax
from jax.experimental import pallas as pl
from jax.experimental.pallas import tpu as pltpu
from jax.sharding import PartitionSpec as P

HD = 128
WINDOW = 5
ROWS = 192


def kernel(count, heads, named, queries, keys, values, out, *scratch):
    windows = (scratch[:heads], scratch[heads : 2 * heads])
    (held_q, held_o, held_w, held_t, local_sem, q_sem, o_sem, y_send, y_recv, sib_send, sib_recv,
     z_send, z_recv, share_send, share_recv) = scratch[2 * heads :]
    sources = (keys, values)
    tiles, tile_len, _ = queries.shape
    slots = named.shape[1]
    rows = min(ROWS, tile_len)
    factor = math.log2(math.e) * HD ** -0.5

    me = lax.axis_index("blk")
    core = lax.rem(me, 2)
    side = lax.rem(me // 2, 2)
    quad = me // 4
    last = count // 4 - 1
    sibling = me + 1 - 2 * core
    partner = me + 2 - 4 * side
    ahead = me + 4 - 8 * side
    can_relay = jnp.where(side == 0, quad < last, quad > 0)
    gets_relay = jnp.where(side == 0, quad > 0, quad < last)
    shares_partner = core == side
    partner_at = 4 - 4 * side
    relay_at = 4 * side

    def pieces(head, which):
        return tiles if which == 1 and head >= heads - 2 else 1

    def part(ref, block, piece=0, total=1):
        size = tiles // total
        return ref.at[pl.ds(block * tiles + piece * size, size)]

    def columns(ref, head, piece=0, total=1):
        size = tiles // total
        return ref.at[pl.ds(piece * size, size), :, pl.ds(head * HD, HD)]

    def local_copy(head, which):
        return pltpu.make_async_copy(
            columns(sources[which], head), part(windows[which][head], 2), local_sem.at[head, which]
        )

    def remote(src, dst, send, recv, target):
        return pltpu.make_async_remote_copy(
            src_ref=src, dst_ref=dst, send_sem=send, recv_sem=recv,
            device_id={"blk": target}, device_id_type=pl.DeviceIdType.MESH,
        )

    def partner_copy(head, which, piece):
        at = (head, which, piece)
        cut = (piece, pieces(head, which))
        return remote(columns(sources[which], head, *cut), part(windows[which][head], relay_at, *cut),
                      y_send.at[at], y_recv.at[at], partner)

    def sibling_copy(head, which):
        at = (head, which)
        return remote(columns(sources[which], head), part(windows[which][head], 1 + 2 * core),
                      sib_send.at[at], sib_recv.at[at], sibling)

    def relay_copy(head, which, piece):
        at = (head, which, piece)
        cut = (piece, pieces(head, which))
        window = windows[which][head]
        return remote(part(window, partner_at, *cut), part(window, relay_at, *cut),
                      z_send.at[at], z_recv.at[at], ahead)

    def share_copy(head, which, piece):
        at = (head, which, piece)
        cut = (piece, pieces(head, which))
        window = windows[which][head]
        return remote(part(window, 4 - 4 * core, *cut), part(window, 3 - 2 * core, *cut),
                      share_send.at[at], share_recv.at[at], sibling)

    def query_copy(head):
        return pltpu.make_async_copy(columns(queries, head), columns(held_q, head), q_sem.at[head])

    def out_copy(head):
        return pltpu.make_async_copy(columns(held_o, head), columns(out, head), o_sem.at[head])

    barrier = pltpu.get_barrier_semaphore()

    def greet(target):
        pl.semaphore_signal(barrier, inc=1, device_id={"blk": target}, device_id_type=pl.DeviceIdType.MESH)

    greet(sibling)
    greet(partner)

    @pl.when(quad > 0)
    def _():
        greet(me - 4)

    @pl.when(quad < last)
    def _():
        greet(me + 4)

    pl.semaphore_wait(barrier, 2 + (quad > 0).astype(jnp.int32) + (quad < last).astype(jnp.int32))

    order = [(head, which) for head in range(heads - 2) for which in range(2)]
    order += [(head, which) for which in range(2) for head in range(heads - 2, heads)]
    for head, which in order:
        for piece in range(pieces(head, which)):
            partner_copy(head, which, piece).start()
        sibling_copy(head, which).start()
        local_copy(head, which).start()
        if which == 0:
            query_copy(head).start()

    def over_rows(step):
        def block(index, carry):
            step(pl.ds(pl.multiple_of(index * rows, rows), rows))
            return carry

        lax.fori_loop(0, tile_len // rows, block, 0)

    def entries(tile):
        base = (me - 2) * tiles
        own = 2 * tiles + tile
        found = []
        for slot in range(slots):
            entry = named[tile, slot]
            ok = entry >= 0
            place = jnp.clip(jnp.where(ok, entry - base, own), 0, WINDOW * tiles - 1)
            found.append((ok, place))
        return found

    def weigh(head, tile, at):
        query = held_q[tile, at, head * HD : (head + 1) * HD]
        found = entries(tile)
        scores = [
            lax.dot_general(query, windows[0][head][place], (((1,), (1,)), ((), ())),
                            preferred_element_type=jnp.float32)
            for _, place in found
        ]
        peaks = [
            jnp.where(ok, jnp.max(score, axis=1, keepdims=True), -jnp.inf)
            for score, (ok, _) in zip(scores, found)
        ]
        top = functools.reduce(jnp.maximum, peaks) * factor
        total = jnp.zeros((rows, 1), jnp.float32)
        for slot, (ok, place) in enumerate(found):
            weights = jnp.exp2(scores[slot] * factor - jnp.where(ok, top, jnp.inf))
            total += jnp.sum(weights, axis=1, keepdims=True)
            yield slot, place, weights.astype(jnp.bfloat16)
        yield total

    def attend(head, tile):
        def step(at):
            summed = jnp.zeros((rows, HD), jnp.float32)
            *parts, total = weigh(head, tile, at)
            for _, place, rounded in parts:
                summed += jnp.dot(rounded, windows[1][head][place], preferred_element_type=jnp.float32)
            held_o[tile, at, head * HD : (head + 1) * HD] = (summed / total).astype(held_o.dtype)

        over_rows(step)

    def score(head, tile):
        late = head - (heads - 2)

        def step(at):
            *parts, total = weigh(head, tile, at)
            for slot, _, rounded in parts:
                held_w[late, tile, at, slot * tile_len : (slot + 1) * tile_len] = rounded
            held_t[late, tile, at, :] = jnp.broadcast_to(total, (rows, HD))

        over_rows(step)

    def gather(head, tile):
        late = head - (heads - 2)

        def step(at):
            summed = jnp.zeros((rows, HD), jnp.float32)
            for slot, (_, place) in enumerate(entries(tile)):
                summed += jnp.dot(
                    held_w[late, tile, at, slot * tile_len : (slot + 1) * tile_len],
                    windows[1][head][place], preferred_element_type=jnp.float32,
                )
            result = summed / held_t[late, tile, at, :]
            held_o[tile, at, head * HD : (head + 1) * HD] = result.astype(held_o.dtype)

        over_rows(step)

    def arrive(head, which, piece=0):
        partner_copy(head, which, piece).wait_recv()

        @pl.when(can_relay)
        def _():
            relay_copy(head, which, piece).start()

        @pl.when(shares_partner)
        def _():
            share_copy(head, which, piece).start()

    def finish(head, which):
        for piece in range(pieces(head, which)):

            @pl.when(gets_relay)
            def _():
                relay_copy(head, which, piece).wait_recv()

                @pl.when(jnp.logical_not(shares_partner))
                def _():
                    share_copy(head, which, piece).start()

    def ready(head, which):
        if which == 0:
            query_copy(head).wait()
        local_copy(head, which).wait()
        sibling_copy(head, which).wait_recv()
        for piece in range(pieces(head, which)):

            @pl.when(jnp.logical_or(jnp.logical_not(shares_partner), gets_relay))
            def _():
                share_copy(head, which, piece).wait_recv()

    half = tiles // 2

    def each(work, head, first):
        for tile in range(half) if first else range(half, tiles):
            work(head, tile)

    def both(head):
        for which in range(2):
            finish(head, which)
        for which in range(2):
            ready(head, which)

    for head in range(heads - 2):
        arrive(head, 0)
        if head > 0:
            both(head - 1)
            each(attend, head - 1, True)
        arrive(head, 1)
        if head > 0:
            each(attend, head - 1, False)
            out_copy(head - 1).start()

    early, late = heads - 2, heads - 1
    arrive(early, 0)
    both(early - 1)
    each(attend, early - 1, True)
    arrive(late, 0)
    finish(early, 0)
    each(attend, early - 1, False)
    out_copy(early - 1).start()
    ready(early, 0)
    for piece in range(tiles):
        arrive(early, 1, piece)
        score(early, piece)
    for piece in range(tiles):
        arrive(late, 1, piece)
        if piece == 0:
            finish(late, 0)
            ready(late, 0)
        if piece == tiles - 1:
            finish(early, 1)
        score(late, piece)
    ready(early, 1)
    for tile in range(tiles):
        gather(early, tile)
    out_copy(early).start()
    finish(late, 1)
    ready(late, 1)
    for tile in range(tiles):
        gather(late, tile)
    out_copy(late).start()

    for head in range(heads):
        out_copy(head).wait()
        for which in range(2):
            sibling_copy(head, which).wait_send()
            for piece in range(pieces(head, which)):
                partner_copy(head, which, piece).wait_send()

                @pl.when(can_relay)
                def _():
                    relay_copy(head, which, piece).wait_send()

                @pl.when(jnp.logical_or(shares_partner, gets_relay))
                def _():
                    share_copy(head, which, piece).wait_send()


def on_device(count, queries, keys, values, neighbours):
    tokens, width = queries.shape
    tiles = neighbours.shape[0]
    tile_len = tokens // tiles
    heads = width // HD
    shape = (tiles, tile_len, width)
    window = pltpu.VMEM((WINDOW * tiles, tile_len, HD), queries.dtype)
    slots = neighbours.shape[1]
    pair = pltpu.SemaphoreType.DMA((heads, 2))
    triple = pltpu.SemaphoreType.DMA((heads, 2, tiles))
    single = pltpu.SemaphoreType.DMA((heads,))
    hbm = pl.BlockSpec(memory_space=pl.ANY)
    out = pl.pallas_call(
        functools.partial(kernel, count, heads),
        out_shape=jax.ShapeDtypeStruct(shape, queries.dtype),
        in_specs=[pl.BlockSpec(memory_space=pltpu.SMEM), hbm, hbm, hbm],
        out_specs=hbm,
        scratch_shapes=[window] * (2 * heads)
        + [pltpu.VMEM(shape, queries.dtype)] * 2
        + [pltpu.VMEM((2, tiles, tile_len, slots * tile_len), queries.dtype)]
        + [pltpu.VMEM((2, tiles, tile_len, HD), jnp.float32)]
        + [pair, single, single, triple, triple, pair, pair]
        + [triple] * 4,
        compiler_params=pltpu.CompilerParams(
            collective_id=0, has_side_effects=True, vmem_limit_bytes=60 * 1024 * 1024
        ),
    )(neighbours, queries.reshape(shape), keys.reshape(shape), values.reshape(shape))
    return out.reshape(tokens, width)


def solution(mesh):
    spec = P(("groups", "blk"), None)
    return jax.shard_map(
        functools.partial(on_device, mesh.shape["blk"]),
        mesh=mesh, in_specs=(spec,) * 4, out_specs=spec, check_vma=False,
    )
```

```python
import functools
import math

import jax
import jax.numpy as jnp
from jax import lax
from jax.experimental import pallas as pl
from jax.experimental.pallas import tpu as pltpu
from jax.sharding import PartitionSpec as P

HD = 128
WINDOW = 5
ROWS = 384


def kernel(count, heads, named, queries, keys, values, out, *scratch):
    windows = (scratch[:heads], scratch[heads : 2 * heads])
    (held_q, held_o, local_sem, q_sem, o_sem, y_send, y_recv, sib_send, sib_recv,
     z_send, z_recv, share_send, share_recv) = scratch[2 * heads :]
    sources = (keys, values)
    tiles, tile_len, _ = queries.shape
    slots = named.shape[1]
    rows = min(ROWS, tile_len)
    factor = math.log2(math.e) * HD ** -0.5

    me = lax.axis_index("blk")
    core = lax.rem(me, 2)
    side = lax.rem(me // 2, 2)
    quad = me // 4
    last = count // 4 - 1
    sibling = me + 1 - 2 * core
    partner = me + 2 - 4 * side
    ahead = me + 4 - 8 * side
    can_relay = jnp.where(side == 0, quad < last, quad > 0)
    gets_relay = jnp.where(side == 0, quad > 0, quad < last)
    shares_partner = core == side
    partner_at = 4 - 4 * side
    relay_at = 4 * side

    def part(ref, block):
        return ref.at[pl.ds(block * tiles, tiles)]

    def columns(ref, head):
        return ref.at[:, :, pl.ds(head * HD, HD)]

    def local_copy(head, which):
        return pltpu.make_async_copy(
            columns(sources[which], head), part(windows[which][head], 2), local_sem.at[head, which]
        )

    def remote(src, dst, send, recv, head, which, target):
        return pltpu.make_async_remote_copy(
            src_ref=src, dst_ref=dst, send_sem=send.at[head, which], recv_sem=recv.at[head, which],
            device_id={"blk": target}, device_id_type=pl.DeviceIdType.MESH,
        )

    def partner_copy(head, which):
        return remote(columns(sources[which], head), part(windows[which][head], relay_at),
                      y_send, y_recv, head, which, partner)

    def sibling_copy(head, which):
        return remote(columns(sources[which], head), part(windows[which][head], 1 + 2 * core),
                      sib_send, sib_recv, head, which, sibling)

    def relay_copy(head, which):
        window = windows[which][head]
        return remote(part(window, partner_at), part(window, relay_at),
                      z_send, z_recv, head, which, ahead)

    def share_copy(head, which):
        window = windows[which][head]
        return remote(part(window, 4 - 4 * core), part(window, 3 - 2 * core),
                      share_send, share_recv, head, which, sibling)

    def query_copy(head):
        return pltpu.make_async_copy(columns(queries, head), columns(held_q, head), q_sem.at[head])

    def out_copy(head):
        return pltpu.make_async_copy(columns(held_o, head), columns(out, head), o_sem.at[head])

    barrier = pltpu.get_barrier_semaphore()

    def greet(target):
        pl.semaphore_signal(barrier, inc=1, device_id={"blk": target}, device_id_type=pl.DeviceIdType.MESH)

    greet(sibling)
    greet(partner)

    @pl.when(quad > 0)
    def _():
        greet(me - 4)

    @pl.when(quad < last)
    def _():
        greet(me + 4)

    pl.semaphore_wait(barrier, 2 + (quad > 0).astype(jnp.int32) + (quad < last).astype(jnp.int32))

    for head in range(heads):
        for which in range(2):
            partner_copy(head, which).start()
        for which in range(2):
            sibling_copy(head, which).start()
            local_copy(head, which).start()
        query_copy(head).start()

    def attend(head, between):
        key_window, value_window = windows[0][head], windows[1][head]
        start = head * HD
        per_tile = tile_len // rows

        def block(index, carry):
            if between is not None:
                pl.when(index == 1)(between)

            tile = index // per_tile
            row = pl.multiple_of(lax.rem(index, per_tile) * rows, rows)
            query = held_q[tile, pl.ds(row, rows), start : start + HD]
            own = 2 * tiles + tile
            base = (me - 2) * tiles
            scores, peaks, valid, places = [], [], [], []
            for slot in range(slots):
                entry = named[tile, slot]
                ok = entry >= 0
                place = jnp.clip(jnp.where(ok, entry - base, own), 0, WINDOW * tiles - 1)
                score = lax.dot_general(
                    query, key_window[place], (((1,), (1,)), ((), ())),
                    preferred_element_type=jnp.float32,
                )
                peak = jnp.max(score, axis=1, keepdims=True)
                peaks.append(jnp.where(ok, peak, -jnp.inf))
                scores.append(score)
                valid.append(ok)
                places.append(place)
            top = functools.reduce(jnp.maximum, peaks) * factor
            total = jnp.zeros((rows, 1), jnp.float32)
            summed = jnp.zeros((rows, HD), jnp.float32)
            for slot in range(slots):
                offset = jnp.where(valid[slot], top, jnp.inf)
                weights = jnp.exp2(scores[slot] * factor - offset)
                total += jnp.sum(weights, axis=1, keepdims=True)
                summed += jnp.dot(
                    weights.astype(jnp.bfloat16), value_window[places[slot]],
                    preferred_element_type=jnp.float32,
                )
            held_o[tile, pl.ds(row, rows), start : start + HD] = (summed / total).astype(held_o.dtype)
            return carry

        lax.fori_loop(0, tiles * per_tile, block, 0)

    def arrive(head, which):
        partner_copy(head, which).wait_recv()

        @pl.when(can_relay)
        def _():
            relay_copy(head, which).start()

        @pl.when(shares_partner)
        def _():
            share_copy(head, which).start()

    for step in range(heads + 1):
        if step < heads:
            arrive(step, 0)
            if step == 0:
                arrive(step, 1)

        if step > 0:
            head = step - 1
            for which in range(2):

                @pl.when(gets_relay)
                def _():
                    relay_copy(head, which).wait_recv()

                    @pl.when(jnp.logical_not(shares_partner))
                    def _():
                        share_copy(head, which).start()

            query_copy(head).wait()
            for which in range(2):
                local_copy(head, which).wait()
                sibling_copy(head, which).wait_recv()

                @pl.when(jnp.logical_or(jnp.logical_not(shares_partner), gets_relay))
                def _():
                    share_copy(head, which).wait_recv()

            attend(head, functools.partial(arrive, step, 1) if step < heads else None)
            out_copy(head).start()

    for head in range(heads):
        out_copy(head).wait()
        for which in range(2):
            partner_copy(head, which).wait_send()
            sibling_copy(head, which).wait_send()

            @pl.when(can_relay)
            def _():
                relay_copy(head, which).wait_send()

            @pl.when(jnp.logical_or(shares_partner, gets_relay))
            def _():
                share_copy(head, which).wait_send()


def on_device(count, queries, keys, values, neighbours):
    tokens, width = queries.shape
    tiles = neighbours.shape[0]
    tile_len = tokens // tiles
    heads = width // HD
    shape = (tiles, tile_len, width)
    window = pltpu.VMEM((WINDOW * tiles, tile_len, HD), queries.dtype)
    pair = pltpu.SemaphoreType.DMA((heads, 2))
    single = pltpu.SemaphoreType.DMA((heads,))
    hbm = pl.BlockSpec(memory_space=pl.ANY)
    out = pl.pallas_call(
        functools.partial(kernel, count, heads),
        out_shape=jax.ShapeDtypeStruct(shape, queries.dtype),
        in_specs=[pl.BlockSpec(memory_space=pltpu.SMEM), hbm, hbm, hbm],
        out_specs=hbm,
        scratch_shapes=[window] * (2 * heads)
        + [pltpu.VMEM(shape, queries.dtype)] * 2
        + [pair, single, single]
        + [pair] * 8,
        compiler_params=pltpu.CompilerParams(
            collective_id=0, has_side_effects=True, vmem_limit_bytes=60 * 1024 * 1024
        ),
    )(neighbours, queries.reshape(shape), keys.reshape(shape), values.reshape(shape))
    return out.reshape(tokens, width)


def solution(mesh):
    spec = P(("groups", "blk"), None)
    return jax.shard_map(
        functools.partial(on_device, mesh.shape["blk"]),
        mesh=mesh, in_specs=(spec,) * 4, out_specs=spec, check_vma=False,
    )
```
